32 devices in a mesh: dp: 8 (over y, x, core), mp: 4 (over z).
Axes of the slice: x: 2, y: 2, z: 4, core: 2. Of those that a mesh axis runs over, the one named last changes fastest.
Arguments:
- segment_ids: int32 [2048], replicated, may hold values from 0 to 1, never falling along the last dimension, each value on 1 to 1536 neighbouring positions
- queries: bfloat16 [2048, 4096], P('dp', 'mp'), may hold values from -45 to 45
- keys: bfloat16 [2048, 512], P('dp'), may hold values from -45 to 45
- values: bfloat16 [2048, 512], P('dp'), may hold values from -6 to 6
- out_weight: bfloat16 [4096, 8192], P('mp'), may hold values from -0.125 to 0.125
Outputs:
- attn_out: bfloat16 [2048, 8192], P('dp', 'mp')
The draws below stay inside these ranges and needn't reach their ends.
Inputs may be any that keep to these rules, and one draw needn't show every extreme that they name: `segment_ids`: rollout numbers never fall along the tokens; every rollout has 1 to 1536 tokens and one has exactly 1536.
All inputs are finite; a program needn't handle non-finite values.
Results may differ from the reference program's by a relative error of at most 0.014.
Values may be sent and summed in bfloat16 or wider, within the bound.
A program may use at most 64 MiB of HBM per device.

```python
import math
import jax
import jax.numpy as jnp
import numpy as np
from jax import lax

D = 8192
HD = 128
QHEADS = 32
KVHEADS = 4
GROUP = 8
TOKENS = 2048
ROLLOUTS = 2
MAXLEN = 1536
N_MP = 4


def shared_pair(key):
    base_keys = jnp.clip(jax.random.normal(jax.random.fold_in(key, 11), (TOKENS, KVHEADS * HD), jnp.float32), -6.0, 6.0)
    base_queries = jnp.clip(jax.random.normal(jax.random.fold_in(key, 12), (TOKENS, QHEADS * HD), jnp.float32), -6.0, 6.0)
    keys_out = base_keys
    queries_out = base_queries
    return (queries_out, keys_out)


def draw_queries(key, part):
    return shared_pair(key)[0].astype(jnp.bfloat16)


def draw_keys(key, part):
    return shared_pair(key)[1].astype(jnp.bfloat16)


def spiked(values, key, source, target, parts, factor):
    def block_of(axis_at):
        return (jnp.arange(values.shape[axis_at]) // (values.shape[axis_at] // parts)).reshape((-1,) + (1,) * (values.ndim - 1 - axis_at))

    first = jax.random.permutation(key, parts)[block_of(target)]
    other_side = (block_of(target) + parts // 2) % parts
    return jnp.where((block_of(source) == first) | (block_of(source) == other_side), factor * values, values)


def level_of(rng, shape, cuts, smallest, top_value):
    gain, own = 1.0, jax.random.fold_in(rng, 6)
    for position, shards_of in cuts:
        steps = jnp.exp(jax.random.uniform(jax.random.fold_in(own, position), (shards_of,), jnp.float32, smallest / len(cuts), top_value / len(cuts)))
        gain = gain * jnp.repeat(steps, shape[position] // shards_of).reshape([-1 if axis == position else 1 for axis in range(len(shape))])
    return gain


def profile(amount, total, limit, skew):
    loads = [(1 << 20) // math.isqrt(rank ** skew) + 1 for rank in range(2, amount + 1)]
    surplus, holding = total - limit - (amount - 1), [1] * (amount - 1)
    while surplus > 0:
        movable = [i for i in range(amount - 1) if holding[i] < limit]
        pool, left = sum([loads[i] for i in movable]), surplus
        for i in movable:
            extra = min(limit - holding[i], max(1, left * loads[i] // pool), surplus)
            holding[i] = holding[i] + extra
            surplus = surplus - extra
    return np.array([limit] + holding)


def uneven(key, number_of, total, reach, lean):
    if number_of == 2:
        one = jax.random.randint(key, (), max(1, total - reach), min(reach, total - 1) + 1)
        return jnp.stack([one, total - one])
    sizes = jnp.asarray(profile(number_of, total, reach, lean), jnp.int32)
    couples = (number_of - 1) // 2
    giver, sink = sizes[1:1 + 2 * couples:2], sizes[2:2 + 2 * couples:2]
    slack = jnp.minimum(giver - 1, reach - sink)
    passed = jax.random.randint(jax.random.fold_in(key, 1), (couples,), 0, 1 << 20) % (slack + 1)
    sizes = sizes.at[1:1 + 2 * couples:2].set(giver - passed).at[2:2 + 2 * couples:2].set(sink + passed)
    return sizes[jax.random.permutation(jax.random.fold_in(key, 2), number_of)]


def centred(own_key, dims, width, limit, cuts=(), kind=jnp.bfloat16):
    factor_of = level_of(own_key, dims, cuts, -0.22, 0.18) if cuts else 1.0
    result = jax.random.normal(own_key, dims, jnp.float32) * width * factor_of
    return jnp.minimum(jnp.maximum(result, -limit), limit).astype(kind)


def gaussian_with(own_key, shape, scale, most, cuts, heavy, kind=jnp.bfloat16):
    array = scale * jax.random.normal(own_key, shape, jnp.float32)
    if cuts:
        array = array * level_of(own_key, shape, cuts, -0.22, 0.18)
    return jnp.clip(spiked(array, jax.random.fold_in(own_key, 3), *heavy), -most, most).astype(kind)


def setup_inputs(seed: int = 0) -> dict:
    seeds = jax.random.split(jax.random.key(seed), 6)
    segment_ids = jnp.searchsorted(jnp.cumsum(uneven(seeds[0], ROLLOUTS, TOKENS, MAXLEN, 2)), jnp.arange(TOKENS), side="right").astype(jnp.int32)
    queries = draw_queries(jax.random.fold_in(seeds[5], 71), 0)
    keys = draw_keys(jax.random.fold_in(seeds[5], 71), 0)
    values = centred(seeds[3], (TOKENS, KVHEADS * HD), 1.0, 6.0, ((0, 8),))
    out_weight = gaussian_with(seeds[4], (QHEADS * HD, D), (QHEADS * HD) ** -0.5, 0.125, ((0, 4),), (0, 1, 4, 2.0))
    return dict(segment_ids=segment_ids, queries=queries, keys=keys, values=values, out_weight=out_weight)


def reference(segment_ids, queries, keys, values, out_weight):
    score_scale = 1.0 / math.sqrt(HD)
    block_len = math.gcd(TOKENS, 512)
    block_count = TOKENS // block_len
    positions = jnp.arange(TOKENS, dtype=jnp.int32)
    key_heads = keys.astype(jnp.float32).reshape(TOKENS, KVHEADS, HD).transpose(1, 0, 2)
    value_heads = values.astype(jnp.float32).reshape(TOKENS, KVHEADS, HD).transpose(1, 0, 2)

    def one_block(block_index):
        offset = (block_index * block_len).astype(jnp.int32)
        query_rows = lax.dynamic_slice_in_dim(queries, offset, block_len, 0).astype(jnp.float32)
        query_rows = query_rows.reshape(block_len, KVHEADS, GROUP, HD).transpose(1, 0, 2, 3)
        seg_rows = lax.dynamic_slice_in_dim(segment_ids, offset, block_len, 0)
        pos_rows = offset + jnp.arange(block_len, dtype=jnp.int32)
        allowed = (seg_rows[:, None] == segment_ids[None, :]) & (positions[None, :] <= pos_rows[:, None])

        def one_group(group_args):
            group_queries, group_keys, group_values = group_args
            scores = jnp.einsum('tjd,sd->tjs', group_queries, group_keys) * score_scale
            scores = jnp.where(allowed[:, None, :], scores, -1e+30)
            row_max = lax.optimization_barrier(jnp.max(scores, axis=-1, keepdims=True))
            weights = jnp.where(allowed[:, None, :], jnp.exp(scores - row_max), 0.0)
            denominator = lax.optimization_barrier(jnp.sum(weights, axis=-1, keepdims=True))
            rounded = lax.optimization_barrier(weights.astype(jnp.bfloat16)).astype(jnp.float32)
            mixed = jnp.einsum('tjs,sd->tjd', rounded, group_values) / denominator
            return mixed.astype(jnp.bfloat16)
        return lax.map(one_group, (query_rows, key_heads, value_heads))
    attended = lax.map(one_block, jnp.arange(block_count, dtype=jnp.int32))
    attended = attended.transpose(0, 2, 1, 3, 4).reshape(TOKENS, QHEADS * HD)
    per_device = QHEADS * HD // N_MP
    head_blocks = attended.reshape(TOKENS, N_MP, per_device).transpose(1, 0, 2)
    weight_blocks = out_weight.reshape(N_MP, per_device, D)

    def add_block(carry, block_args):
        block_rows, block_weight = block_args
        partial_value = jnp.dot(block_rows, block_weight, preferred_element_type=jnp.float32)
        rounded = lax.optimization_barrier(partial_value.astype(jnp.bfloat16)).astype(jnp.float32)
        return (carry + rounded, None)
    summed, unused = lax.scan(add_block, jnp.zeros((TOKENS, D), jnp.float32), (head_blocks, weight_blocks))
    return summed.astype(jnp.bfloat16)
```

```python
import functools
import math

import jax
import jax.numpy as jnp
from jax import lax
from jax.experimental import pallas as pl
from jax.experimental.pallas import tpu as pltpu
from jax.sharding import PartitionSpec as P

HD = 128
GROUP = 8
MESH = pl.DeviceIdType.MESH


def kernel(
    n_dp, n_mp, key_span, chunk,
    seg_ref, q_ref, k_hbm, v_hbm, w_hbm, out_ref,
    kv, w, bias, attended, from_left, from_right, to_right, to_left,
    load_sems, w_sem, kv_send, kv_recv, pass_send, pass_recv,
    right_send, right_recv, left_send, left_recv,
):
    rows = q_ref.shape[0]
    heads = q_ref.shape[1] // HD
    tokens = n_dp * rows
    out_cols = out_ref.shape[1]
    pieces = out_cols // chunk
    chips = n_dp // 2
    dp, mp = lax.axis_index("dp"), lax.axis_index("mp")
    core, chip = dp % 2, dp // 2
    partner = dp + 1 - 2 * core
    first_row = pl.multiple_of(dp * rows, rows)

    kv_col = pl.multiple_of((mp * heads // GROUP) * HD, HD)
    own = kv.at[:, pl.ds(first_row, rows), :]
    loads = [
        pltpu.make_async_copy(
            src.at[:, pl.ds(kv_col, HD)], kv.at[i, pl.ds(first_row, rows), :], load_sems.at[i]
        )
        for i, src in enumerate((k_hbm, v_hbm))
    ]
    for copy in loads:
        copy.start()
    w_copy = pltpu.make_async_copy(w_hbm, w, w_sem)
    w_copy.start()

    barrier = pltpu.get_barrier_semaphore()
    for r in range(1, chips):
        peer = ((chip + r) % chips) * 2 + core
        pl.semaphore_signal(barrier, inc=1, device_id={"dp": peer}, device_id_type=MESH)
    pl.semaphore_signal(barrier, inc=1, device_id={"dp": partner}, device_id_type=MESH)

    @pl.when(mp > 0)
    def _():
        pl.semaphore_signal(barrier, inc=1, device_id={"mp": mp - 1}, device_id_type=MESH)

    @pl.when(mp < n_mp - 1)
    def _():
        pl.semaphore_signal(barrier, inc=1, device_id={"mp": mp + 1}, device_id_type=MESH)

    ends = jnp.where(mp == 0, 1, 0) + jnp.where(mp == n_mp - 1, 1, 0)
    for copy in loads:
        copy.wait()
    pl.semaphore_wait(barrier, chips + 2 - ends)

    def kv_copy(block, send_sem, recv_sem, target):
        part = kv.at[:, pl.ds(pl.multiple_of(block * rows, rows), rows), :]
        return pltpu.make_async_remote_copy(
            src_ref=part, dst_ref=part, send_sem=send_sem, recv_sem=recv_sem,
            device_id={"dp": target}, device_id_type=MESH,
        )

    sends = [
        kv_copy(dp, kv_send.at[r], kv_recv.at[r], ((chip + r) % chips) * 2 + core)
        for r in range(1, chips)
    ]
    sends.append(kv_copy(dp, pass_send.at[0], pass_recv.at[0], partner))
    for copy in sends:
        copy.start()

    own_segs = seg_ref[:, pl.ds(first_row, rows)].astype(jnp.float32)
    diagonal = lax.broadcasted_iota(jnp.int32, (rows, rows), 0) == lax.broadcasted_iota(
        jnp.int32, (rows, rows), 1
    )
    query_segs = jnp.sum(
        jnp.where(diagonal, jnp.broadcast_to(own_segs, (rows, rows)), 0.0), axis=1, keepdims=True
    )
    for start in range(0, tokens, key_span):
        key_segs = seg_ref[:, start : start + key_span].astype(jnp.float32)
        key_pos = start + lax.broadcasted_iota(jnp.int32, (rows, key_span), 1)
        query_pos = first_row + lax.broadcasted_iota(jnp.int32, (rows, key_span), 0)
        allowed = (query_segs == key_segs) & (key_pos <= query_pos)
        bias[:, start : start + key_span] = jnp.where(allowed, 0.0, -1e30)

    for r in range(1, chips):
        source = ((chip + chips - r) % chips) * 2 + core
        kv_copy(source, kv_send.at[r], kv_recv.at[r], dp).wait_recv()
        forward = kv_copy(source, pass_send.at[r], pass_recv.at[r], partner)
        forward.start()
        sends.append(forward)
    for r in range(chips):
        source = ((chip + chips - r) % chips) * 2 + 1 - core
        kv_copy(source, pass_send.at[r], pass_recv.at[r], dp).wait_recv()

    scale = math.log2(math.e) / math.sqrt(HD)

    def one_head(h, carry):
        columns = pl.ds(pl.multiple_of(h * HD, HD), HD)
        q = q_ref[:, columns]
        top = total = acc = None
        for start in range(0, tokens, key_span):
            span = slice(start, start + key_span)
            scores = lax.dot_general(
                q, kv[0, span, :], (((1,), (1,)), ((), ())), preferred_element_type=jnp.float32
            )
            scores = scores * scale + bias[:, span]
            new_top = jnp.max(scores, axis=1, keepdims=True)
            if top is not None:
                new_top = jnp.maximum(top, new_top)
            probs = jnp.exp2(scores - new_top)
            part_sum = jnp.sum(probs, axis=1, keepdims=True)
            part = jnp.dot(
                probs.astype(jnp.bfloat16), kv[1, span, :], preferred_element_type=jnp.float32
            )
            if top is None:
                total, acc = part_sum, part
            else:
                fade = jnp.exp2(top - new_top)
                total, acc = total * fade + part_sum, acc * fade + part
            top = new_top
        attended[:, columns] = (acc / total).astype(jnp.bfloat16)
        return carry

    lax.fori_loop(0, heads, one_head, 0)
    w_copy.wait()

    def project(d, k):
        columns = pl.ds(pl.multiple_of(d * out_cols + k * chunk, chunk), chunk)
        return jnp.dot(attended[...], w[:, columns], preferred_element_type=jnp.float32)

    def right_copy(d, k):
        at = d * pieces + k
        return pltpu.make_async_remote_copy(
            src_ref=to_right.at[at], dst_ref=from_left.at[at],
            send_sem=right_send.at[at], recv_sem=right_recv.at[at],
            device_id={"mp": mp + 1}, device_id_type=MESH,
        )

    def left_copy(d, k):
        at = d * pieces + k
        return pltpu.make_async_remote_copy(
            src_ref=to_left.at[at], dst_ref=from_right.at[at],
            send_sem=left_send.at[at], recv_sem=left_recv.at[at],
            device_id={"mp": mp - 1}, device_id_type=MESH,
        )

    def relay(d, k, copy_of, staged, arrived, at_end):
        at = d * pieces + k
        value = project(d, k)

        @pl.when(at_end)
        def _():
            staged[at] = value.astype(jnp.bfloat16)

        @pl.when(jnp.logical_not(at_end))
        def _():
            copy_of(d, k).wait_recv()
            staged[at] = (value + arrived[at].astype(jnp.float32)).astype(jnp.bfloat16)

        copy_of(d, k).start()

    def step(i, carry):
        s, k = i // pieces, i % pieces

        @pl.when(n_mp - 1 - s > mp)
        def _():
            relay(n_mp - 1 - s, k, right_copy, to_right, from_left, mp == 0)

        @pl.when(s < mp)
        def _():
            relay(s, k, left_copy, to_left, from_right, mp == n_mp - 1)

        return carry

    lax.fori_loop(0, (n_mp - 1) * pieces, step, 0)

    def finish(k, carry):
        at = mp * pieces + k
        columns = pl.ds(pl.multiple_of(k * chunk, chunk), chunk)
        value = project(mp, k)

        @pl.when(mp == 0)
        def _():
            left_copy(mp, k).wait_recv()
            out_ref[:, columns] = (value + from_right[at].astype(jnp.float32)).astype(jnp.bfloat16)

        @pl.when(mp == n_mp - 1)
        def _():
            right_copy(mp, k).wait_recv()
            out_ref[:, columns] = (value + from_left[at].astype(jnp.float32)).astype(jnp.bfloat16)

        @pl.when((mp > 0) & (mp < n_mp - 1))
        def _():
            left_copy(mp, k).wait_recv()
            right_copy(mp, k).wait_recv()
            both = from_left[at].astype(jnp.float32) + from_right[at].astype(jnp.float32)
            out_ref[:, columns] = (value + both).astype(jnp.bfloat16)

        return carry

    lax.fori_loop(0, pieces, finish, 0)

    for copy in sends:
        copy.wait_send()

    def drain(i, carry):
        s, k = i // pieces, i % pieces

        @pl.when(n_mp - 1 - s > mp)
        def _():
            right_copy(n_mp - 1 - s, k).wait_send()

        @pl.when(s < mp)
        def _():
            left_copy(s, k).wait_send()

        return carry

    lax.fori_loop(0, (n_mp - 1) * pieces, drain, 0)


def solution(mesh):
    n_dp, n_mp = mesh.shape["dp"], mesh.shape["mp"]

    def on_device(segment_ids, queries, keys, values, out_weight):
        rows, tokens = queries.shape[0], segment_ids.shape[0]
        depth, width = out_weight.shape
        out_cols = width // n_mp
        chunk = min(256, out_cols)
        slots = n_mp * (out_cols // chunk)
        key_span = min(2048, tokens)
        dma = pltpu.SemaphoreType.DMA
        vmem = pl.BlockSpec(memory_space=pltpu.VMEM)
        hbm = pl.BlockSpec(memory_space=pl.ANY)
        stage = pltpu.VMEM((slots, rows, chunk), jnp.bfloat16)
        return pl.pallas_call(
            functools.partial(kernel, n_dp, n_mp, key_span, chunk),
            out_shape=jax.ShapeDtypeStruct((rows, out_cols), jnp.bfloat16),
            in_specs=[vmem, vmem, hbm, hbm, hbm],
            out_specs=vmem,
            scratch_shapes=[
                pltpu.VMEM((2, tokens, HD), jnp.bfloat16),
                pltpu.VMEM((depth, width), jnp.bfloat16),
                pltpu.VMEM((rows, tokens), jnp.float32),
                pltpu.VMEM((rows, queries.shape[1]), jnp.bfloat16),
                stage, stage, stage, stage,
                dma((2,)), dma,
                dma((n_dp // 2,)), dma((n_dp // 2,)), dma((n_dp // 2,)), dma((n_dp // 2,)),
                dma((slots,)), dma((slots,)), dma((slots,)), dma((slots,)),
            ],
            compiler_params=pltpu.CompilerParams(
                collective_id=0, has_side_effects=True, vmem_limit_bytes=60 * 1024 * 1024
            ),
        )(segment_ids.reshape(1, tokens), queries, keys, values, out_weight)

    return jax.shard_map(
        on_device,
        mesh=mesh,
        in_specs=(P(), P("dp", "mp"), P("dp", None), P("dp", None), P("mp", None)),
        out_specs=P("dp", "mp"),
        check_vma=False,
    )
```

```python
import functools
import math

import jax
import jax.numpy as jnp
from jax import lax
from jax.experimental import pallas as pl
from jax.experimental.pallas import tpu as pltpu
from jax.sharding import PartitionSpec as P

HD = 128
GROUP = 8
LAG = 2
MESH = pl.DeviceIdType.MESH


def kernel(
    n_dp, n_mp, key_span, chunk,
    seg_ref, q_ref, k_hbm, v_hbm, w_hbm, out_ref,
    kv, w, bias, attended, from_left, from_right, to_right, to_left,
    load_sems, w_sem, kv_send, kv_recv, pass_send, pass_recv,
    right_send, right_recv, left_send, left_recv,
):
    rows = q_ref.shape[0]
    heads = q_ref.shape[1] // HD
    tokens = n_dp * rows
    out_cols = out_ref.shape[1]
    pieces = out_cols // chunk
    chips = n_dp // 2
    dp, mp = lax.axis_index("dp"), lax.axis_index("mp")
    core, chip = dp % 2, dp // 2
    partner = dp + 1 - 2 * core
    first_row = pl.multiple_of(dp * rows, rows)

    kv_col = pl.multiple_of((mp * heads // GROUP) * HD, HD)
    own = kv.at[:, pl.ds(first_row, rows), :]
    loads = [
        pltpu.make_async_copy(
            src.at[:, pl.ds(kv_col, HD)], kv.at[i, pl.ds(first_row, rows), :], load_sems.at[i]
        )
        for i, src in enumerate((k_hbm, v_hbm))
    ]
    for copy in loads:
        copy.start()
    w_copy = pltpu.make_async_copy(w_hbm, w, w_sem)
    w_copy.start()

    barrier = pltpu.get_barrier_semaphore()
    for r in range(1, chips):
        peer = ((chip + r) % chips) * 2 + core
        pl.semaphore_signal(barrier, inc=1, device_id={"dp": peer}, device_id_type=MESH)
    pl.semaphore_signal(barrier, inc=1, device_id={"dp": partner}, device_id_type=MESH)

    @pl.when(mp > 0)
    def _():
        pl.semaphore_signal(barrier, inc=1, device_id={"mp": mp - 1}, device_id_type=MESH)

    @pl.when(mp < n_mp - 1)
    def _():
        pl.semaphore_signal(barrier, inc=1, device_id={"mp": mp + 1}, device_id_type=MESH)

    ends = jnp.where(mp == 0, 1, 0) + jnp.where(mp == n_mp - 1, 1, 0)
    for copy in loads:
        copy.wait()
    pl.semaphore_wait(barrier, chips + 2 - ends)

    def kv_copy(block, send_sem, recv_sem, target):
        part = kv.at[:, pl.ds(pl.multiple_of(block * rows, rows), rows), :]
        return pltpu.make_async_remote_copy(
            src_ref=part, dst_ref=part, send_sem=send_sem, recv_sem=recv_sem,
            device_id={"dp": target}, device_id_type=MESH,
        )

    sends = [
        kv_copy(dp, kv_send.at[r], kv_recv.at[r], ((chip + r) % chips) * 2 + core)
        for r in range(1, chips)
    ]
    sends.append(kv_copy(dp, pass_send.at[0], pass_recv.at[0], partner))
    for copy in sends:
        copy.start()

    own_segs = seg_ref[:, pl.ds(first_row, rows)].astype(jnp.float32)
    diagonal = lax.broadcasted_iota(jnp.int32, (rows, rows), 0) == lax.broadcasted_iota(
        jnp.int32, (rows, rows), 1
    )
    query_segs = jnp.sum(
        jnp.where(diagonal, jnp.broadcast_to(own_segs, (rows, rows)), 0.0), axis=1, keepdims=True
    )
    for start in range(0, tokens, key_span):
        key_segs = seg_ref[:, start : start + key_span].astype(jnp.float32)
        key_pos = start + lax.broadcasted_iota(jnp.int32, (rows, key_span), 1)
        query_pos = first_row + lax.broadcasted_iota(jnp.int32, (rows, key_span), 0)
        allowed = (query_segs == key_segs) & (key_pos <= query_pos)
        bias[:, start : start + key_span] = jnp.where(allowed, 0.0, -1e30)

    for r in range(1, chips):
        source = ((chip + chips - r) % chips) * 2 + core
        kv_copy(source, kv_send.at[r], kv_recv.at[r], dp).wait_recv()
        forward = kv_copy(source, pass_send.at[r], pass_recv.at[r], partner)
        forward.start()
        sends.append(forward)
    for r in range(chips):
        source = ((chip + chips - r) % chips) * 2 + 1 - core
        kv_copy(source, pass_send.at[r], pass_recv.at[r], dp).wait_recv()

    scale = math.log2(math.e) / math.sqrt(HD)

    def one_head(h, carry):
        columns = pl.ds(pl.multiple_of(h * HD, HD), HD)
        q = q_ref[:, columns]
        top = total = acc = None
        for start in range(0, tokens, key_span):
            span = slice(start, start + key_span)
            scores = lax.dot_general(
                q, kv[0, span, :], (((1,), (1,)), ((), ())), preferred_element_type=jnp.float32
            )
            scores = scores * scale + bias[:, span]
            new_top = jnp.max(scores, axis=1, keepdims=True)
            if top is not None:
                new_top = jnp.maximum(top, new_top)
            probs = jnp.exp2(scores - new_top)
            part_sum = jnp.sum(probs, axis=1, keepdims=True)
            part = jnp.dot(
                probs.astype(jnp.bfloat16), kv[1, span, :], preferred_element_type=jnp.float32
            )
            if top is None:
                total, acc = part_sum, part
            else:
                fade = jnp.exp2(top - new_top)
                total, acc = total * fade + part_sum, acc * fade + part
            top = new_top
        attended[:, columns] = (acc / total).astype(jnp.bfloat16)
        return carry

    lax.fori_loop(0, heads, one_head, 0)
    w_copy.wait()

    def project(d, k):
        columns = pl.ds(pl.multiple_of(d * out_cols + k * chunk, chunk), chunk)
        return jnp.dot(attended[...], w[:, columns], preferred_element_type=jnp.float32)

    def right_copy(d, k):
        at = d * pieces + k
        return pltpu.make_async_remote_copy(
            src_ref=to_right.at[at], dst_ref=from_left.at[at],
            send_sem=right_send.at[at], recv_sem=right_recv.at[at],
            device_id={"mp": mp + 1}, device_id_type=MESH,
        )

    def left_copy(d, k):
        at = d * pieces + k
        return pltpu.make_async_remote_copy(
            src_ref=to_left.at[at], dst_ref=from_right.at[at],
            send_sem=left_send.at[at], recv_sem=left_recv.at[at],
            device_id={"mp": mp - 1}, device_id_type=MESH,
        )

    def relay(d, k, copy_of, staged, arrived, at_end):
        at = d * pieces + k
        value = project(d, k)

        @pl.when(at_end)
        def _():
            staged[at] = value.astype(jnp.bfloat16)

        @pl.when(jnp.logical_not(at_end))
        def _():
            copy_of(d, k).wait_recv()
            staged[at] = (value + arrived[at].astype(jnp.float32)).astype(jnp.bfloat16)

        copy_of(d, k).start()

    items = (n_mp - 1) * pieces

    def step(t, carry):
        right_item = t - LAG * mp
        left_item = t - LAG * (n_mp - 1 - mp)
        right_at = jnp.maximum(right_item, 0)
        left_at = jnp.maximum(left_item, 0)
        right_to = n_mp - 1 - right_at // pieces
        left_to = left_at // pieces

        @pl.when((right_item >= 0) & (right_item < items) & (right_to > mp))
        def _():
            relay(right_to, right_at % pieces, right_copy, to_right, from_left, mp == 0)

        @pl.when((left_item >= 0) & (left_item < items) & (left_to < mp))
        def _():
            relay(left_to, left_at % pieces, left_copy, to_left, from_right, mp == n_mp - 1)

        return carry

    lax.fori_loop(0, items + LAG * (n_mp - 1), step, 0)

    def finish(k, carry):
        at = mp * pieces + k
        columns = pl.ds(pl.multiple_of(k * chunk, chunk), chunk)
        value = project(mp, k)

        @pl.when(mp == 0)
        def _():
            left_copy(mp, k).wait_recv()
            out_ref[:, columns] = (value + from_right[at].astype(jnp.float32)).astype(jnp.bfloat16)

        @pl.when(mp == n_mp - 1)
        def _():
            right_copy(mp, k).wait_recv()
            out_ref[:, columns] = (value + from_left[at].astype(jnp.float32)).astype(jnp.bfloat16)

        @pl.when((mp > 0) & (mp < n_mp - 1))
        def _():
            left_copy(mp, k).wait_recv()
            right_copy(mp, k).wait_recv()
            both = from_left[at].astype(jnp.float32) + from_right[at].astype(jnp.float32)
            out_ref[:, columns] = (value + both).astype(jnp.bfloat16)

        return carry

    lax.fori_loop(0, pieces, finish, 0)

    for copy in sends:
        copy.wait_send()

    def drain(i, carry):
        s, k = i // pieces, i % pieces

        @pl.when(n_mp - 1 - s > mp)
        def _():
            right_copy(n_mp - 1 - s, k).wait_send()

        @pl.when(s < mp)
        def _():
            left_copy(s, k).wait_send()

        return carry

    lax.fori_loop(0, (n_mp - 1) * pieces, drain, 0)


def solution(mesh):
    n_dp, n_mp = mesh.shape["dp"], mesh.shape["mp"]

    def on_device(segment_ids, queries, keys, values, out_weight):
        rows, tokens = queries.shape[0], segment_ids.shape[0]
        depth, width = out_weight.shape
        out_cols = width // n_mp
        chunk = min(256, out_cols)
        slots = n_mp * (out_cols // chunk)
        key_span = min(2048, tokens)
        dma = pltpu.SemaphoreType.DMA
        vmem = pl.BlockSpec(memory_space=pltpu.VMEM)
        hbm = pl.BlockSpec(memory_space=pl.ANY)
        stage = pltpu.VMEM((slots, rows, chunk), jnp.bfloat16)
        return pl.pallas_call(
            functools.partial(kernel, n_dp, n_mp, key_span, chunk),
            out_shape=jax.ShapeDtypeStruct((rows, out_cols), jnp.bfloat16),
            in_specs=[vmem, vmem, hbm, hbm, hbm],
            out_specs=vmem,
            scratch_shapes=[
                pltpu.VMEM((2, tokens, HD), jnp.bfloat16),
                pltpu.VMEM((depth, width), jnp.bfloat16),
                pltpu.VMEM((rows, tokens), jnp.float32),
                pltpu.VMEM((rows, queries.shape[1]), jnp.bfloat16),
                stage, stage, stage, stage,
                dma((2,)), dma,
                dma((n_dp // 2,)), dma((n_dp // 2,)), dma((n_dp // 2,)), dma((n_dp // 2,)),
                dma((slots,)), dma((slots,)), dma((slots,)), dma((slots,)),
            ],
            compiler_params=pltpu.CompilerParams(
                collective_id=0, has_side_effects=True, vmem_limit_bytes=60 * 1024 * 1024
            ),
        )(segment_ids.reshape(1, tokens), queries, keys, values, out_weight)

    return jax.shard_map(
        on_device,
        mesh=mesh,
        in_specs=(P(), P("dp", "mp"), P("dp", None), P("dp", None), P("mp", None)),
        out_specs=P("dp", "mp"),
        check_vma=False,
    )
```
